32 devices in a mesh: expert: 8 (over y, x, core), replica: 4 (over z).
Axes of the slice: x: 2, y: 2, z: 4, core: 2. Of those that a mesh axis runs over, the one named last changes fastest.
Arguments:
- tokens: bfloat16 [16384, 2048], P(('expert', 'replica')), may hold values from -6 to 6
- d_hidden: bfloat16 [16384, 768], P(('expert', 'replica')), may hold values from -6 to 6
- w_gate: bfloat16 [32, 2048, 768], P(None, ('expert', 'replica')), may hold values from -0.125 to 0.125
- w_up: bfloat16 [32, 2048, 768], P(None, ('expert', 'replica')), may hold values from -0.125 to 0.125
- expert_ids: int32 [32], replicated, may hold values from 0 to 31
Outputs:
- hidden: bfloat16 [16384, 768], P(('expert', 'replica'))
- token_grad: bfloat16 [16384, 2048], P(('expert', 'replica'))
- grad_gate: bfloat16 [32, 2048, 768], P(None, ('expert', 'replica'))
- grad_up: bfloat16 [32, 2048, 768], P(None, ('expert', 'replica'))
The draws below stay inside these ranges and needn't reach their ends.
Inputs may be any that keep to these rules, and one draw needn't show every extreme that they name: expert_ids[b] is the expert used by the rows of block b; several blocks may use the same expert.
All inputs are finite; a program needn't handle non-finite values.
Results may differ from the reference program's by a relative error of at most 0.0057.
Values may be sent and summed in bfloat16 or wider, within the bound.
A program may use at most 128 MiB of HBM per device.

```python
import math
import jax
import jax.numpy as jnp
import numpy as np
from jax import lax

D = 2048
FF = 768
TOK_DEV = 512
EXPERTS = 32
BLOCKS = 32
ROWS = 16384


def with_ends(result, own_key, low, largest):
    dims = result.shape
    place = [jax.random.randint(jax.random.fold_in(own_key, axis), (), 0, dims[axis]) for axis in range(len(dims))]
    result = result.at[tuple(place)].set(low)
    longest = dims.index(max(dims))
    place[longest] = (place[longest] + 1) % dims[longest]
    return result.at[tuple(place)].set(largest)


def shard_levels(stream_key, dims, pieces, low, largest):
    gain, own = 1.0, jax.random.fold_in(stream_key, 6)
    for position, parts in pieces:
        draws = jnp.exp(jax.random.uniform(jax.random.fold_in(own, position), (parts,), jnp.float32, low / len(pieces), largest / len(pieces)))
        gain = gain * jnp.repeat(draws, dims[position] // parts).reshape([-1 if axis == position else 1 for axis in range(len(dims))])
    return gain


def rank_bounds(number_of, skew):
    loads = [(1 << 20) // math.isqrt(grade ** skew) + 1 for grade in range(1, number_of + 1)]
    spread = 1 + sum(loads) // (1 << 30)
    return np.cumsum(np.array([max(1, weight // spread) for weight in loads]))


def ranked(own_key, shape, number_of, skew):
    table = rank_bounds(number_of, skew)
    pick = jax.random.randint(jax.random.fold_in(own_key, 1), shape, 0, int(table[number_of - 1]))
    grade = jnp.searchsorted(jnp.asarray(table, jnp.int32), pick, side="right")
    return jax.random.permutation(jax.random.fold_in(own_key, 2), number_of)[grade].astype(jnp.int32)


def gaussian(own_key, dims, width, bound, pieces=(), dtype=jnp.bfloat16):
    drawn = width * jax.random.normal(own_key, dims, jnp.float32)
    if pieces:
        drawn = drawn * shard_levels(own_key, dims, pieces, -0.22, 0.18)
    return jnp.clip(drawn, -bound, bound).astype(dtype)


def setup_inputs(seed: int = 0) -> dict:
    arg_keys = jax.random.split(jax.random.key(seed), 6)
    return {
        "tokens": gaussian(arg_keys[0], (ROWS, D), 1.0, 6.0, ((0, 32),)),
        "d_hidden": gaussian(arg_keys[1], (ROWS, FF), 1.0, 6.0, ((0, 32),)),
        "w_gate": gaussian(arg_keys[2], (EXPERTS, D, FF), D ** -0.5, 0.125, ((1, 32),)),
        "w_up": gaussian(arg_keys[3], (EXPERTS, D, FF), D ** -0.5, 0.125, ((1, 32),)),
        "expert_ids": with_ends(ranked(arg_keys[4], (BLOCKS,), EXPERTS, 2), jax.random.fold_in(arg_keys[4], 3), 0, EXPERTS - 1).astype(jnp.int32),
    }


def reference(tokens, d_hidden, w_gate, w_up, expert_ids):
    count = expert_ids.shape[0]
    token_blocks = tokens.reshape(count, TOK_DEV, D)
    grad_blocks = d_hidden.reshape(count, TOK_DEV, FF)
    scale = TOK_DEV ** -0.5

    def step(carry, item):
        acc_gate, acc_up = carry
        rows, upstream_bf, which = item
        gate_whole = w_gate[which]
        up_whole = w_up[which]
        gate_pre = jnp.dot(rows, gate_whole, preferred_element_type=jnp.float32)
        up_pre = jnp.dot(rows, up_whole, preferred_element_type=jnp.float32)
        sigmoid_gate = jax.nn.sigmoid(gate_pre)
        activated = gate_pre * sigmoid_gate
        hidden_block = (activated * up_pre).astype(jnp.bfloat16)
        upstream = upstream_bf.astype(jnp.float32)
        d_gate = (upstream * up_pre * sigmoid_gate * (1.0 + gate_pre * (1.0 - sigmoid_gate))).astype(jnp.bfloat16)
        d_up = (upstream * activated).astype(jnp.bfloat16)
        token_block = (jnp.dot(d_gate, gate_whole.T, preferred_element_type=jnp.float32)
                       + jnp.dot(d_up, up_whole.T, preferred_element_type=jnp.float32)).astype(jnp.bfloat16)
        part_gate = jnp.dot(rows.T, d_gate, preferred_element_type=jnp.float32).astype(jnp.bfloat16)
        part_up = jnp.dot(rows.T, d_up, preferred_element_type=jnp.float32).astype(jnp.bfloat16)
        part_gate = lax.optimization_barrier(part_gate).astype(jnp.float32)
        part_up = lax.optimization_barrier(part_up).astype(jnp.float32)
        acc_gate = lax.dynamic_update_index_in_dim(acc_gate, acc_gate[which] + part_gate, which, 0)
        acc_up = lax.dynamic_update_index_in_dim(acc_up, acc_up[which] + part_up, which, 0)
        return (acc_gate, acc_up), (hidden_block, token_block)

    start = (jnp.zeros(w_gate.shape, jnp.float32), jnp.zeros(w_up.shape, jnp.float32))
    (acc_gate, acc_up), (hidden_blocks, token_blocks_out) = lax.scan(
        step, start, (token_blocks, grad_blocks, expert_ids))
    hidden = hidden_blocks.reshape(tokens.shape[0], FF)
    token_grad = token_blocks_out.reshape(tokens.shape[0], D)
    grad_gate = (acc_gate * scale).astype(jnp.bfloat16)
    grad_up = (acc_up * scale).astype(jnp.bfloat16)
    return hidden, token_grad, grad_gate, grad_up
```

```python
import functools

import jax
import jax.numpy as jnp
from jax import lax
from jax.experimental import pallas as pl
from jax.experimental.pallas import tpu as pltpu
from jax.sharding import PartitionSpec as P

MESH = pl.DeviceIdType.MESH
ANY = pl.BlockSpec(memory_space=pl.ANY)
BF16 = jnp.bfloat16
F32 = jnp.float32


def chunk_count(width):
    for chunks in (3, 2):
        if width % (chunks * 128) == 0:
            return chunks
    return 1


def pick_kernel(step_blocks, chunks, ids_ref, gate_ref, up_ref, out_ref, sem):
    first = pl.program_id(0) * step_blocks
    width = out_ref.shape[3] // 2
    copies = []
    for i in range(step_blocks):
        which = ids_ref[first + i]
        for c in range(chunks):
            for half, source in enumerate((gate_ref, up_ref)):
                copies.append(
                    pltpu.make_async_copy(
                        source.at[which, :, pl.ds(c * width, width)],
                        out_ref.at[c, i, :, pl.ds(half * width, width)],
                        sem.at[i, c, half],
                    )
                )
    for copy in copies:
        copy.start()
    for copy in copies:
        copy.wait()


def pick(w_gate, w_up, expert_ids, chunks):
    blocks = expert_ids.shape[0]
    _, rows, hidden = w_gate.shape
    both = 2 * hidden // chunks
    step_blocks = 8
    return pl.pallas_call(
        functools.partial(pick_kernel, step_blocks, chunks),
        grid_spec=pltpu.PrefetchScalarGridSpec(
            num_scalar_prefetch=1,
            grid=(blocks // step_blocks,),
            in_specs=[ANY, ANY],
            out_specs=pl.BlockSpec(
                (chunks, step_blocks, rows, both), lambda s, ids: (0, s, 0, 0)
            ),
            scratch_shapes=[pltpu.SemaphoreType.DMA((step_blocks, chunks, 2))],
        ),
        out_shape=jax.ShapeDtypeStruct((chunks, blocks, rows, both), BF16),
    )(expert_ids, w_gate, w_up)


def main_kernel(
    owners,
    members,
    chunks,
    rows,
    tok_hbm,
    dh_hbm,
    out_w,
    hid_hbm,
    tg_hbm,
    terms,
    tok,
    tok_t,
    dh,
    hid,
    wbuf,
    part,
    dcat,
    acc,
    tg,
    load_sem,
    own_sem,
    w_send,
    w_recv,
    g_send,
    g_recv,
    out_sem,
):
    total = owners * members
    e = lax.axis_index("expert")
    z = lax.axis_index("replica")
    me = e * members + z
    tokens_n, model = tok.shape
    both = wbuf.shape[3]
    width = both // 2
    half = members // 2

    def partner(k):
        i = k // members
        j = (k % members + half) % members
        pe = (e + i) % owners
        pz = (z + j) % members
        return pe, pz, pe * members + pz

    def source_of(k):
        i = k // members
        j = (k % members + half) % members
        se = (e + owners - i) % owners
        sz = (z + members - j) % members
        return se, sz, se * members + sz

    def each_other(fn):
        @pl.loop(0, half)
        def _(k):
            fn(k)

        @pl.loop(half + 1, total)
        def _(k):
            fn(k)

    loads = [
        pltpu.make_async_copy(tok_hbm, tok, load_sem.at[0]),
        pltpu.make_async_copy(dh_hbm, dh, load_sem.at[1]),
    ]
    for copy in loads:
        copy.start()

    barrier = pltpu.get_barrier_semaphore()

    def greet(k):
        pe, pz, _ = partner(k)
        pl.semaphore_signal(barrier, inc=1, device_id=(pe, pz), device_id_type=MESH)

    each_other(greet)
    pl.semaphore_wait(barrier, total - 1)

    def w_copy(c, k):
        pe, pz, p = partner(k)
        return pltpu.make_async_remote_copy(
            src_ref=out_w.at[c, p],
            dst_ref=wbuf.at[c, me],
            send_sem=w_send.at[c, k],
            recv_sem=w_recv.at[c, k],
            device_id=(pe, pz),
            device_id_type=MESH,
        )

    def g_copy(c, k):
        pe, pz, p = partner(k)
        return pltpu.make_async_remote_copy(
            src_ref=part.at[c, p],
            dst_ref=terms.at[c, me],
            send_sem=g_send.at[c, k],
            recv_sem=g_recv.at[c, k],
            device_id=(pe, pz),
            device_id_type=MESH,
        )

    for c in range(chunks):
        each_other(lambda k, c=c: w_copy(c, k).start())
        pltpu.make_async_copy(out_w.at[c, me], wbuf.at[c, me], own_sem.at[0, c]).start()

    for copy in loads:
        copy.wait()
    tile = 256
    for r in range(model // tile):
        tok_t[r * tile : (r + 1) * tile, :] = tok[:, r * tile : (r + 1) * tile].T

    per_tile = tile // rows
    for c in range(chunks):
        cols = slice(c * width, (c + 1) * width)
        pltpu.make_async_copy(out_w.at[c, me], wbuf.at[c, me], own_sem.at[0, c]).wait()
        each_other(lambda k, c=c: w_copy(c, k).wait_recv())
        weights = wbuf.at[c]

        @pl.loop(0, tokens_n // tile)
        def _(r, c=c, cols=cols):
            at = pl.ds(pl.multiple_of(r * tile, tile), tile)
            pre = jnp.dot(
                tok[at, :],
                wbuf[c].reshape(model, both),
                preferred_element_type=F32,
            )
            gate, up = pre[:, :width], pre[:, width:]
            s = jax.nn.sigmoid(gate)
            activated = gate * s
            upstream = dh[at, cols].astype(F32)
            hid[at, cols] = (activated * up).astype(BF16)
            dcat[at, :width] = (upstream * up * s * (1.0 + gate * (1.0 - s))).astype(BF16)
            dcat[at, width:] = (upstream * activated).astype(BF16)

        @pl.loop(0, model // tile)
        def _(r, c=c):
            at = pl.ds(pl.multiple_of(r * tile, tile), tile)
            out = jnp.dot(tok_t[at, :], dcat[...], preferred_element_type=F32)
            part[c, pl.ds(r * per_tile, per_tile)] = out.astype(BF16).reshape(
                per_tile, rows, both
            )

        each_other(lambda k, c=c: g_copy(c, k).start())
        pltpu.make_async_copy(part.at[c, me], terms.at[c, me], own_sem.at[1, c]).start()

        @pl.loop(0, model // tile)
        def _(r, c=c):
            at = pl.ds(pl.multiple_of(r * tile, tile), tile)
            piece = wbuf[c, pl.ds(r * per_tile, per_tile)].reshape(tile, both)
            out = lax.dot_general(
                dcat[...], piece, (((1,), (1,)), ((), ())), preferred_element_type=F32
            )
            if c > 0:
                out = out + acc[r]
            if c == chunks - 1:
                tg[:, at] = out.astype(BF16)
            else:
                acc[r] = out

    outs = [
        pltpu.make_async_copy(hid, hid_hbm, out_sem.at[0]),
        pltpu.make_async_copy(tg, tg_hbm, out_sem.at[1]),
    ]
    for copy in outs:
        copy.start()
    for copy in outs:
        copy.wait()
    for c in range(chunks):
        each_other(lambda k, c=c: w_copy(c, k).wait_send())
        pltpu.make_async_copy(part.at[c, me], terms.at[c, me], own_sem.at[1, c]).wait()
        each_other(lambda k, c=c: g_copy(c, k).wait_send())
        each_other(lambda k, c=c: g_copy(c, k).wait_recv())


def exchange(tokens, d_hidden, out_w, owners, members):
    chunks, total, rows, both = out_w.shape
    tokens_n, model = tokens.shape
    hidden = d_hidden.shape[1]
    return pl.pallas_call(
        functools.partial(main_kernel, owners, members, chunks, rows),
        in_specs=[ANY, ANY, ANY],
        out_specs=[ANY, ANY, ANY],
        out_shape=[
            jax.ShapeDtypeStruct((tokens_n, hidden), BF16),
            jax.ShapeDtypeStruct((tokens_n, model), BF16),
            jax.ShapeDtypeStruct((chunks, total, rows, both), BF16),
        ],
        scratch_shapes=[
            pltpu.VMEM((tokens_n, model), BF16),
            pltpu.VMEM((model, tokens_n), BF16),
            pltpu.VMEM((tokens_n, hidden), BF16),
            pltpu.VMEM((tokens_n, hidden), BF16),
            pltpu.VMEM((chunks, total, rows, both), BF16),
            pltpu.VMEM((chunks, total, rows, both), BF16),
            pltpu.VMEM((tokens_n, both), BF16),
            pltpu.VMEM((model // 256, tokens_n, 256), F32),
            pltpu.VMEM((tokens_n, model), BF16),
            pltpu.SemaphoreType.DMA((2,)),
            pltpu.SemaphoreType.DMA((2, chunks)),
            pltpu.SemaphoreType.DMA((chunks, total)),
            pltpu.SemaphoreType.DMA((chunks, total)),
            pltpu.SemaphoreType.DMA((chunks, total)),
            pltpu.SemaphoreType.DMA((chunks, total)),
            pltpu.SemaphoreType.DMA((2,)),
        ],
        compiler_params=pltpu.CompilerParams(collective_id=0, has_side_effects=True),
    )(tokens, d_hidden, out_w)


def sum_kernel(scale, spread_ref, terms_ref, gate_ref, up_ref):
    _, blocks, group, both = terms_ref.shape
    experts = gate_ref.shape[0]
    width = both // 2
    flat = terms_ref[0].reshape(blocks * group, both)
    out = jnp.dot(spread_ref[...], flat, preferred_element_type=F32) * scale
    out = out.astype(BF16)
    gate_ref[...] = out[:, :width].reshape(experts, group, width)
    up_ref[...] = out[:, width:].reshape(experts, group, width)


def sum_terms(terms, expert_ids, experts, scale):
    chunks, blocks, rows, both = terms.shape
    width = both // 2
    group = min(rows, 16)
    selector = expert_ids[None, :] == jnp.arange(experts, dtype=jnp.int32)[:, None]
    unit = jnp.arange(group)[:, None] == jnp.arange(group)[None, :]
    spread = (selector[:, None, :, None] & unit[None, :, None, :]).astype(BF16)
    spread = spread.reshape(experts * group, blocks * group)
    result = jax.ShapeDtypeStruct((experts, rows, chunks * width), BF16)
    block = pl.BlockSpec((experts, group, width), lambda c, r: (0, r, c))
    return pl.pallas_call(
        functools.partial(sum_kernel, scale),
        grid=(chunks, rows // group),
        in_specs=[
            pl.BlockSpec((experts * group, blocks * group), lambda c, r: (0, 0)),
            pl.BlockSpec((1, blocks, group, both), lambda c, r: (c, 0, r, 0)),
        ],
        out_specs=[block, block],
        out_shape=[result, result],
    )(spread, terms)


def per_device(tokens, d_hidden, w_gate, w_up, expert_ids):
    owners = lax.axis_size("expert")
    members = lax.axis_size("replica")
    chunks = chunk_count(w_gate.shape[2])
    out_w = pick(w_gate, w_up, expert_ids, chunks)
    hidden, token_grad, terms = exchange(tokens, d_hidden, out_w, owners, members)
    scale = tokens.shape[0] ** (-0.5)
    grad_gate, grad_up = sum_terms(terms, expert_ids, w_gate.shape[0], scale)
    return hidden, token_grad, grad_gate, grad_up


def solution(mesh):
    both_axes = ("expert", "replica")
    in_specs = (
        P(both_axes, None),
        P(both_axes, None),
        P(None, both_axes, None),
        P(None, both_axes, None),
        P(),
    )
    out_specs = (
        P(both_axes, None),
        P(both_axes, None),
        P(None, both_axes, None),
        P(None, both_axes, None),
    )
    return jax.shard_map(
        per_device, mesh=mesh, in_specs=in_specs, out_specs=out_specs, check_vma=False
    )
```
